32 devices in a mesh: gx: 4 (over y, x), gy: 4 (over z), gz: 2 (over core).
Axes of the slice: x: 2, y: 2, z: 4, core: 2. Of those that a mesh axis runs over, the one named last changes fastest.
Arguments:
- position: float32 [4096, 3, 128], P(('gx', 'gy', 'gz')), may hold values from 0 to 4, as said below
- velocity: float32 [4096, 3, 128], P(('gx', 'gy', 'gz')), may hold values from -0.3 to 0.3
- particle_mass: float32 [4096, 128], P(('gx', 'gy', 'gz')), may hold values from 0.001953125 to 0.0078125
- send_first: int32 [32, 32, 4], P(('gx', 'gy', 'gz')), may hold values from -1 to 127, as said below
- neighbours_first: int32 [4096, 16], P(('gx', 'gy', 'gz')), may hold values from 0 to 255, as said below
- destination: int32 [4096], P(('gx', 'gy', 'gz')), may hold values from 0 to 4095, as said below
- send_second: int32 [32, 32, 4], P(('gx', 'gy', 'gz')), may hold values from -1 to 127, as said below
- neighbours_second: int32 [4096, 16], P(('gx', 'gy', 'gz')), may hold values from 0 to 255, as said below
Outputs:
- position_out: float32 [4096, 3, 128], P(('gx', 'gy', 'gz'))
- velocity_out: float32 [4096, 3, 128], P(('gx', 'gy', 'gz'))
- density_out: float32 [4096, 128], P(('gx', 'gy', 'gz'))
The draws below stay inside these ranges and needn't reach their ends.
Inputs may be any that keep to these rules, and one draw needn't show every extreme that they name: The particles of a block owned by the device at grid position (i_gx, i_gy, i_gz) lie in its box [i_gx, i_gx + 1] x [i_gy, i_gy + 1] x [i_gz, i_gz + 1], all of one block within a cube of side 1/2. `send_first`: only devices whose grid positions along gx, gy and gz differ by at most one in each (and are not the same) send ghosts to each other. The filled slots of one pair come first and hold distinct blocks; some pair fills all 4 slots. `send_second`: as for send_first, in the new layout. `neighbours_first`: entries name only the device's own blocks or filled ghost slots of send_first; the entries of a block are distinct and never the block itself. `neighbours_second`: entries name only the device's own blocks or filled ghost slots of send_second; the entries of a block are distinct and never the block itself. `destination`: A permutation of the 4096 positions; a block stays or moves to a device next to its owner along exactly one of gx, gy, gz; at most 2 blocks go from one device to another, and some pairs move exactly 2.
All inputs are finite; a program needn't handle non-finite values.
Results may differ from the reference program's by a relative error of at most 0.0001.
Values sent between devices are 32-bit elements; how exact they have to be, the bound alone decides.
A program may use at most 128 MiB of HBM per device.

```python
import math
import jax
import jax.numpy as jnp
from jax import lax

PARTICLES = 128
NEIGHBOURS = 16
BLOCKS = 128
GHOST_CAP = 4
MOVE_CAP = 2
ALL_BLOCKS = 4096
N_GX = 4
N_GY = 4
N_GZ = 2


def grid_places():
    devices = N_GX * N_GY * N_GZ
    index = jnp.arange(devices, dtype=jnp.int32)
    along = (index // (N_GY * N_GZ), index // N_GZ % N_GY, index % N_GZ)
    return (index, along)


def block_cells(key):
    index, along = grid_places()
    devices = N_GX * N_GY * N_GZ
    scores = jax.random.randint(jax.random.fold_in(key, 21), (devices, BLOCKS), 0, 1 << 14) * BLOCKS
    ordered = jnp.argsort(scores + jnp.arange(BLOCKS, dtype=jnp.int32)[None, :], axis=1).astype(jnp.int32)
    octant = ordered % 8
    first = 2 * along[0][:, None] + octant // 4
    second = 2 * along[1][:, None] + octant // 2 % 2
    third = 2 * along[2][:, None] + octant % 2
    return jnp.stack([first, second, third], axis=2).astype(jnp.int32)


def draw_destination(key, part):
    base = jax.random.fold_in(key, 13)
    index, along = grid_places()
    devices = N_GX * N_GY * N_GZ
    extents = (N_GX, N_GY, N_GZ)
    strides = (N_GY * N_GZ, N_GZ, 1)
    cells = block_cells(key)
    block_index = jnp.arange(BLOCKS, dtype=jnp.int32)
    target = index[:, None] * BLOCKS + block_index[None, :]
    taken = jnp.zeros((devices, BLOCKS), jnp.int32)
    for rounds in range(6):
        axis_number = rounds // 2
        parity = rounds % 2
        place = along[axis_number]
        partner_place = jnp.where((place - parity) % 2 == 0, place + 1, place - 1)
        exists = (partner_place >= 0) & (partner_place < extents[axis_number])
        partner = jnp.clip(index + (partner_place - place) * strides[axis_number], 0, devices - 1)
        local_cell = cells[:, :, axis_number] - 2 * place[:, None]
        facing = jnp.where((partner_place > place)[:, None], local_cell == 1, local_cell == 0)
        ranking = jax.random.randint(jax.random.fold_in(base, 20 + rounds), (devices, BLOCKS), 0, 1 << 14) * BLOCKS
        ranking = ranking + block_index[None, :] + jnp.where(facing, 0, 1 << 28) + taken * (1 << 29)
        picked = jnp.argsort(ranking, axis=1).astype(jnp.int32)[:, :MOVE_CAP]
        amount = jax.random.randint(jax.random.fold_in(base, rounds + 1), (devices,), 1, MOVE_CAP + 1)
        if rounds == 0:
            amount = jnp.full((devices,), MOVE_CAP, jnp.int32)
        pair_amount = amount[jnp.minimum(index, partner)]
        for offset in range(MOVE_CAP):
            mine = picked[:, offset]
            theirs = picked[partner, offset]
            active = exists & (offset < pair_amount)
            target = target.at[index, mine].set(jnp.where(active, partner * BLOCKS + theirs, target[index, mine]))
            taken = taken.at[index, mine].set(jnp.maximum(taken[index, mine], active.astype(jnp.int32)))
    return target.reshape(devices * BLOCKS).astype(jnp.int32)


def moved_cells(key):
    cells = block_cells(key)
    devices = N_GX * N_GY * N_GZ
    destination = draw_destination(key, 0)
    flat = jnp.zeros((devices * BLOCKS, 3), jnp.int32).at[destination].set(cells.reshape(devices * BLOCKS, 3))
    return flat.reshape(devices, BLOCKS, 3)


def ghost_tables(key, which, cells):
    base = jax.random.fold_in(key, which)
    index, along = grid_places()
    devices = N_GX * N_GY * N_GZ
    near = (jnp.abs(along[0][:, None] - along[0][None, :]) <= 1) & (jnp.abs(along[1][:, None] - along[1][None, :]) <= 1)
    near = near & (jnp.abs(along[2][:, None] - along[2][None, :]) <= 1) & (index[:, None] != index[None, :])
    corner = jnp.stack(along, axis=1)
    lower = 2 * corner - 1
    upper = 2 * corner + 2
    eligible = (cells[:, None, :, :] >= lower[None, :, None, :]) & (cells[:, None, :, :] <= upper[None, :, None, :])
    eligible = jnp.all(eligible, axis=3)
    reach = jnp.sum(eligible.astype(jnp.int32), axis=2)
    amount = jax.random.randint(jax.random.fold_in(base, 1), (devices, devices), 1, GHOST_CAP + 1)
    forced = (index[:, None] == 1) & (index[None, :] == 0) | (index[:, None] == 0) & (index[None, :] == 1)
    amount = jnp.minimum(jnp.where(forced, GHOST_CAP, amount), reach) * near.astype(jnp.int32)
    block_index = jnp.arange(BLOCKS, dtype=jnp.int32)
    scores = jax.random.randint(jax.random.fold_in(base, 2), (devices, devices, BLOCKS), 0, 1 << 14) * BLOCKS
    scores = scores + block_index[None, None, :] + jnp.where(eligible, 0, 1 << 28)
    chosen = jnp.argsort(scores, axis=2).astype(jnp.int32)[:, :, :GHOST_CAP]
    slot_index = jnp.arange(GHOST_CAP, dtype=jnp.int32)
    sender = jnp.where(slot_index[None, None, :] < amount[:, :, None], chosen, -1).astype(jnp.int32)
    received = jnp.transpose(sender, (1, 0, 2))
    ghost_cell = cells[index[None, :, None], jnp.maximum(received, 0)]
    entry_cells = jnp.concatenate([cells, ghost_cell.reshape(devices, devices * GHOST_CAP, 3)], axis=1)
    filled = jnp.concatenate([jnp.ones((devices, BLOCKS), bool), (received >= 0).reshape(devices, devices * GHOST_CAP)], axis=1)
    width = BLOCKS + devices * GHOST_CAP
    entry_index = jnp.arange(width, dtype=jnp.int32)
    adjacent = filled[:, None, :] & jnp.ones((devices, BLOCKS, width), bool)
    for axis_number in range(3):
        spacing = cells[:, :, None, axis_number] - entry_cells[:, None, :, axis_number]
        adjacent = adjacent & (jnp.abs(spacing) <= 1)
    host_score = jax.random.randint(jax.random.fold_in(base, 3), (devices, BLOCKS, width), 0, 1 << 14) * BLOCKS
    host_score = host_score + block_index[None, :, None] + jnp.where(adjacent, 1 << 28, 0)
    host_block = jnp.argsort(host_score, axis=1).astype(jnp.int32)[:, BLOCKS - 1, :]
    designated = (block_index[None, :, None] == host_block[:, None, :]) & adjacent & (entry_index >= BLOCKS)[None, None, :]
    own_entry = entry_index[None, None, :] == block_index[None, :, None]
    entry_class = jnp.where(designated, 0, jnp.where(adjacent, 1, 2))
    entry_class = jnp.where(jnp.logical_not(filled)[:, None, :], 3, entry_class)
    entry_class = jnp.where(own_entry, 4, entry_class)
    ranking = jax.random.randint(jax.random.fold_in(base, 4), (devices, BLOCKS, width), 0, 1 << 12) * width
    ranking = entry_class * (1 << 26) + ranking + entry_index[None, None, :]
    entries = jnp.argsort(ranking, axis=2).astype(jnp.int32)[:, :, :NEIGHBOURS]
    return (sender, entries.reshape(devices * BLOCKS, NEIGHBOURS).astype(jnp.int32))


def draw_position(key, part):
    devices = N_GX * N_GY * N_GZ
    cells = block_cells(key).reshape(devices * BLOCKS, 3).astype(jnp.float32)
    base = jax.random.fold_in(key, 22)
    shape = (devices * BLOCKS, 3, PARTICLES)
    jitter = jax.random.uniform(jax.random.fold_in(base, 1), shape, jnp.float32)
    return ((cells[:, :, None] + jitter) * 0.5).astype(jnp.float32)


def draw_send_first(key, part):
    return ghost_tables(key, 11, block_cells(key))[0]


def draw_neighbours_first(key, part):
    return ghost_tables(key, 11, block_cells(key))[1]


def draw_send_second(key, part):
    return ghost_tables(key, 12, moved_cells(key))[0]


def draw_neighbours_second(key, part):
    return ghost_tables(key, 12, moved_cells(key))[1]


def block_scale(key, dims, cuts, least, top_value):
    level = 1.0
    for dim, shards_of in cuts:
        heights = jax.random.uniform(jax.random.fold_in(jax.random.fold_in(key, 6), dim), (shards_of,), jnp.float32, least / len(cuts), top_value / len(cuts))
        level = level * jnp.repeat(jnp.exp(heights), dims[dim] // shards_of).reshape((-1,) + (1,) * (len(dims) - 1 - dim))
    return level


def setup_inputs(seed: int = 0) -> dict:
    splits = jax.random.split(jax.random.key(seed), 9)
    position = draw_position(jax.random.fold_in(splits[8], 71), 0)
    velocity = jnp.clip(jax.random.uniform(splits[1], (ALL_BLOCKS, 3, PARTICLES), jnp.float32, -0.3, 0.3) * block_scale(splits[1], (ALL_BLOCKS, 3, PARTICLES), ((0, 32),), -0.4, 0.0), -0.3, 0.3)
    particle_mass = jnp.clip(jnp.exp(math.log(0.0078125) - 1.3862944 * jax.random.uniform(splits[2], (ALL_BLOCKS, PARTICLES), jnp.float32) ** block_scale(splits[2], (ALL_BLOCKS, PARTICLES), ((0, 32),), -0.2, 0.2)), 0.001953125, 0.0078125)
    send_first = draw_send_first(jax.random.fold_in(splits[8], 71), 0)
    neighbours_first = draw_neighbours_first(jax.random.fold_in(splits[8], 71), 0)
    destination = draw_destination(jax.random.fold_in(splits[8], 71), 0)
    send_second = draw_send_second(jax.random.fold_in(splits[8], 71), 0)
    neighbours_second = draw_neighbours_second(jax.random.fold_in(splits[8], 71), 0)
    return {"position": position, "velocity": velocity, "particle_mass": particle_mass, "send_first": send_first, "neighbours_first": neighbours_first, "destination": destination, "send_second": send_second, "neighbours_second": neighbours_second}


smooth_len = 0.5
time_step = 0.25


def pair_density(home_points, away_points, away_mass):
    offset = home_points[:, :, :, None] - away_points[:, :, None, :]
    squared = jnp.sum(offset * offset, axis=1)
    kernel = jnp.maximum(1.0 - squared / (smooth_len * smooth_len), 0.0)
    return jnp.sum(away_mass[:, None, :] * (kernel * kernel * kernel), axis=2)


def pair_force(home_points, home_term, away_points, away_mass, away_term):
    offset = home_points[:, :, :, None] - away_points[:, :, None, :]
    squared = jnp.sum(offset * offset, axis=1)
    kernel = jnp.maximum(1.0 - squared / (smooth_len * smooth_len), 0.0)
    weight = away_mass[:, None, :] * (home_term[:, :, None] + away_term[:, None, :]) * kernel * kernel
    return (6.0 / (smooth_len * smooth_len)) * jnp.sum(weight[:, None, :, :] * offset, axis=3)


def pressure_term(density):
    return jnp.exp(jnp.log(density) * (-1.0 / 3.0))


def table_density(home_points, home_mass, all_points, all_mass, lookup):
    initial = pair_density(home_points, home_points, home_mass)

    def add_column(column, running):
        picked = lookup[:, column]
        return running + pair_density(home_points, all_points[picked], all_mass[picked])

    return lax.fori_loop(0, lookup.shape[1], add_column, initial)


def table_force(home_points, home_mass, home_term, all_points, all_mass, all_term, lookup):
    initial = pair_force(home_points, home_term, home_points, home_mass, home_term)

    def add_column(column, running):
        picked = lookup[:, column]
        return running + pair_force(home_points, home_term, all_points[picked], all_mass[picked], all_term[picked])

    return lax.fori_loop(0, lookup.shape[1], add_column, initial)


def global_rows(sender, neighbours):
    total_blocks = neighbours.shape[0]
    owner_device = jnp.arange(total_blocks, dtype=jnp.int32) // BLOCKS
    remote = jnp.maximum(neighbours - BLOCKS, 0)
    source = remote // GHOST_CAP
    within = remote % GHOST_CAP
    listed = sender[source, owner_device[:, None], within]
    far_row = jnp.where(listed >= 0, source * BLOCKS + listed, total_blocks)
    return jnp.where(neighbours < BLOCKS, owner_device[:, None] * BLOCKS + neighbours, far_row).astype(jnp.int32)


def sph_forces(points, weights, sender, neighbours):
    total_blocks = points.shape[0]
    groups = total_blocks // BLOCKS
    lookup = global_rows(sender, neighbours)
    all_points = jnp.concatenate([points, jnp.zeros((1,) + points.shape[1:], jnp.float32)], axis=0)
    all_mass = jnp.concatenate([weights, jnp.zeros((1, weights.shape[1]), jnp.float32)], axis=0)
    grouped_points = points.reshape((groups, BLOCKS) + points.shape[1:])
    grouped_mass = weights.reshape(groups, BLOCKS, weights.shape[1])
    grouped_rows = lookup.reshape(groups, BLOCKS, lookup.shape[1])

    def density_group(packed):
        return table_density(packed[0], packed[1], all_points, all_mass, packed[2])

    density = lax.map(density_group, (grouped_points, grouped_mass, grouped_rows)).reshape(weights.shape)
    all_rho = jnp.concatenate([density, jnp.ones((1, density.shape[1]), jnp.float32)], axis=0)
    all_term = pressure_term(all_rho)
    grouped_term = all_term[:total_blocks].reshape(groups, BLOCKS, weights.shape[1])

    def force_group(packed):
        return table_force(packed[0], packed[1], packed[3], all_points, all_mass, all_term, packed[2])

    acceleration = lax.map(force_group, (grouped_points, grouped_mass, grouped_rows, grouped_term)).reshape(points.shape)
    return density, acceleration


def reference(position, velocity, particle_mass, send_first, neighbours_first, destination, send_second, neighbours_second):
    density, acceleration = sph_forces(position, particle_mass, send_first, neighbours_first)
    velocity = velocity + time_step * acceleration
    position = position + time_step * velocity
    position = jnp.zeros_like(position).at[destination].set(position)
    velocity = jnp.zeros_like(velocity).at[destination].set(velocity)
    moved_mass = jnp.zeros_like(particle_mass).at[destination].set(particle_mass)
    density, acceleration = sph_forces(position, moved_mass, send_second, neighbours_second)
    velocity = velocity + time_step * acceleration
    position = position + time_step * velocity
    return position, velocity, density
```

```python
import jax
import jax.numpy as jnp
import numpy as np
from jax import lax
from jax.experimental import pallas as pl
from jax.experimental.pallas import tpu as pltpu
from jax.sharding import PartitionSpec as P

MOVE_CAP = 2


smooth_len = 0.5
time_step = 0.25


def padded_2(block, sides, width):
    for axis, dim in sides:
        count = lax.axis_size(axis)
        forward = [(i, i + 1) for i in range(count - 1)]
        backward = [(target, source) for source, target in forward]
        low = lax.ppermute(
            lax.slice_in_dim(block, block.shape[dim] - width, None, axis=dim), axis, forward
        )
        high = lax.ppermute(lax.slice_in_dim(block, 0, width, axis=dim), axis, backward)
        block = jnp.concatenate([low, block, high], axis=dim)
    return block


def pressure_term(density):
    return jnp.exp(jnp.log(density) * (-1.0 / 3.0))


PART_PAIRS = ((0, 0), (0, 1), (1, 0), (0, 2), (2, 0), (1, 1))
INVERSE = 1.0 / (smooth_len * smooth_len)


def three_parts(value):
    parts = []
    for _ in range(3):
        part = value.astype(jnp.bfloat16).astype(jnp.float32)
        parts.append(part)
        value = value - part
    return parts


def cube_root(mass):
    return jnp.exp(jnp.log(mass) * (1.0 / 3.0))


def density_kernel(lookup, stacked, out, home, away):
    blocks, columns = lookup.shape

    def prepare(r, carry):
        tile = stacked[r]
        here = tile[0:3]
        root = cube_root(tile[3:4])
        square = jnp.sum(here * here, axis=0, keepdims=True)
        one = jnp.ones_like(square)
        blank = jnp.zeros_like(here)
        far = jnp.concatenate(
            [2.0 * INVERSE * root * here, -INVERSE * root * square, root, blank], axis=0
        )
        near = jnp.concatenate([here, one, 1.0 - INVERSE * square, blank], axis=0)
        far_parts = three_parts(far)
        near_parts = three_parts(near)
        rows = jnp.concatenate([far_parts[a] for a, _ in PART_PAIRS], axis=0)
        away[r] = rows.T.astype(jnp.bfloat16)
        home[r] = jnp.concatenate([near_parts[b] for _, b in PART_PAIRS], axis=0).astype(
            jnp.bfloat16
        )
        return carry

    lax.fori_loop(0, stacked.shape[0], prepare, 0, unroll=4)

    def one_block(b, carry):
        rhs = home[b]
        acc = jnp.zeros((8, rhs.shape[1]), jnp.float32)
        for k in range(columns + 1):
            row = b if k == 0 else lookup[b, k - 1]
            w = jnp.dot(away[row], rhs, preferred_element_type=jnp.float32)
            w = jnp.maximum(w, 0.0)
            w = w * w * w
            acc = acc + jnp.sum(w.reshape(w.shape[0] // 8, 8, w.shape[1]), axis=0)
        out[pl.ds(b, 1), :] = jnp.sum(acc, axis=0, keepdims=True)
        return carry

    lax.fori_loop(0, blocks, one_block, 0)


def force_kernel(lookup, home, away, stacked, term, out, moment):
    blocks, columns = lookup.shape

    def prepare(r, carry):
        tile = stacked[r]
        root = cube_root(tile[3:4])
        q = term[pl.ds(r, 1), :]
        plain = jnp.concatenate([root, root * tile[0:3]], axis=0)
        full = jnp.concatenate([plain, plain * q], axis=0)
        high = full.astype(jnp.bfloat16).astype(jnp.float32)
        moment[r] = jnp.concatenate([high, full - high], axis=0).astype(jnp.bfloat16)
        return carry

    lax.fori_loop(0, stacked.shape[0], prepare, 0, unroll=4)

    def one_block(b, carry):
        rhs = home[b]
        acc = jnp.zeros((16, 2 * rhs.shape[1]), jnp.float32)
        rows = [b] + [lookup[b, k] for k in range(columns)]
        for start in range(0, columns + 1, GROUP):
            group = rows[start : start + GROUP]
            parts = []
            for row in group:
                w = jnp.dot(away[row], rhs, preferred_element_type=jnp.float32)
                w = jnp.maximum(w, 0.0)
                w = w * w
                high = w.astype(jnp.bfloat16)
                low = (w - high.astype(jnp.float32)).astype(jnp.bfloat16)
                parts.append(jnp.concatenate([high, low], axis=1))
            feature = jnp.concatenate([moment[row] for row in group], axis=1)
            both = jnp.concatenate(parts, axis=0)
            acc = acc + jnp.dot(feature, both, preferred_element_type=jnp.float32)
        acc = acc[:, : rhs.shape[1]] + acc[:, rhs.shape[1] :]
        sums = acc[0:8] + acc[8:16]
        q = term[pl.ds(b, 1), :]
        here = stacked[b][0:3]
        near = here * sums[0:1] - sums[1:4]
        far = here * sums[4:5] - sums[5:8]
        out[b] = 6.0 * INVERSE * (q * near + far)
        return carry

    lax.fori_loop(0, blocks, one_block, 0)


GROUP = 2


def kernel_call(body, out_shape, operands, scratch=()):
    vmem = pl.BlockSpec(memory_space=pltpu.VMEM)
    smem = pl.BlockSpec(memory_space=pltpu.SMEM)
    return pl.pallas_call(
        body,
        out_shape=out_shape,
        in_specs=[smem] + [vmem] * (len(operands) - 1),
        out_specs=jax.tree.map(lambda _: vmem, out_shape),
        scratch_shapes=scratch,
    )(*operands)


def pair_sums(stacked, lookup, finish_term):
    blocks = lookup.shape[0]
    total, _, width = stacked.shape
    depth = 8 * len(PART_PAIRS)
    density, home, away = kernel_call(
        density_kernel,
        (
            jax.ShapeDtypeStruct((blocks, width), jnp.float32),
            jax.ShapeDtypeStruct((total, depth, width), jnp.bfloat16),
            jax.ShapeDtypeStruct((total, width, depth), jnp.bfloat16),
        ),
        (lookup, stacked),
    )
    all_term = finish_term(density)
    acceleration = kernel_call(
        force_kernel,
        jax.ShapeDtypeStruct((blocks, 3, width), jnp.float32),
        (lookup, home, away, stacked, all_term),
        [pltpu.VMEM((total, 16, width), jnp.bfloat16)],
    )
    return (density, acceleration)


def near_slots(sender_rows):
    size_x = lax.axis_size("gx")
    size_y = lax.axis_size("gy")
    size_z = lax.axis_size("gz")
    shifts = np.array(
        [
            [first, second, third]
            for first in (-1, 0, 1)
            for second in (-1, 0, 1)
            for third in (-1, 0, 1)
        ],
        dtype=np.int32,
    )
    target_x = lax.axis_index("gx") + shifts[:, 0]
    target_y = lax.axis_index("gy") + shifts[:, 1]
    target_z = lax.axis_index("gz") + shifts[:, 2]
    inside = (target_x >= 0) & (target_x < size_x) & (target_y >= 0) & (target_y < size_y)
    inside = inside & (target_z >= 0) & (target_z < size_z)
    target = (target_x * size_y + target_y) * size_z + target_z
    picked = sender_rows[jnp.clip(target, 0, sender_rows.shape[0] - 1)]
    return jnp.where(inside[:, None], picked, -1)


def fill_slots(payload, sender_rows, blank):
    usable = sender_rows >= 0
    gathered = payload[jnp.maximum(sender_rows, 0)]
    broadcast_shape = usable.shape + (1,) * (payload.ndim - 1)
    return jnp.where(usable.reshape(broadcast_shape), gathered, blank)


def ghost_blocks(payload, sender_rows):
    buffer = fill_slots(payload, near_slots(sender_rows), 0.0)
    cube = buffer.reshape((3, 3, 3) + buffer.shape[1:])
    padded = padded_2(cube, (("gx", 0), ("gy", 1), ("gz", 2)), 1)
    return padded[0::2, 0::2, 0::2].reshape((-1,) + payload.shape[1:])


def ghost_density(density, sender_rows):
    buffer = fill_slots(density, near_slots(sender_rows), 1.0)
    cube = buffer.reshape((3, 3, 3) + buffer.shape[1:])
    padded = padded_2(cube, (("gx", 0), ("gy", 1), ("gz", 2)), 1)
    return padded[0::2, 0::2, 0::2].reshape((-1,) + density.shape[1:])


def table_rows(neighbours, blocks, ghost_cap):
    size_y = lax.axis_size("gy")
    size_z = lax.axis_size("gz")
    remote = jnp.maximum(neighbours - blocks, 0)
    source = remote // ghost_cap
    within = remote % ghost_cap
    code = (source // (size_y * size_z) - lax.axis_index("gx") + 1) * 9
    code = code + (source // size_z % size_y - lax.axis_index("gy") + 1) * 3
    code = code + (source % size_z - lax.axis_index("gz") + 1)
    return jnp.where(neighbours < blocks, neighbours, blocks + code * ghost_cap + within)


def sph_forces(points, weights, sender_rows, neighbours):
    blocks = points.shape[0]
    payload = jnp.concatenate([points, weights[:, None, :]], axis=1)
    stacked = jnp.concatenate([payload, ghost_blocks(payload, sender_rows)], axis=0)
    lookup = table_rows(neighbours, blocks, sender_rows.shape[1])
    middle = [lax.axis_index(axis).astype(jnp.float32) + 0.5 for axis in ("gx", "gy", "gz")]
    middle = jnp.stack(middle + [jnp.float32(0.0)])
    stacked = stacked - middle[None, :, None]

    def finish_term(density):
        all_rho = jnp.concatenate([density, ghost_density(density, sender_rows)], axis=0)
        return pressure_term(all_rho)

    return pair_sums(stacked, lookup, finish_term)


def migrate(fields, destination):
    blocks = fields.shape[0]
    width = fields.shape[2]
    myself = lax.axis_index(("gx", "gy", "gz"))
    owner_device = destination // blocks
    new_place = destination % blocks
    moving = owner_device != myself
    label_row = (
        jnp.zeros((blocks, 1, width), jnp.float32)
        .at[:, 0, 0]
        .set((new_place + 1).astype(jnp.float32))
    )
    carried = jnp.concatenate([fields, label_row], axis=1)
    staying = (
        jnp.zeros_like(fields).at[jnp.where(moving, blocks, new_place)].set(fields, mode="drop")
    )
    size_y = lax.axis_size("gy")
    size_z = lax.axis_size("gz")
    delta_x = owner_device // (size_y * size_z) - lax.axis_index("gx")
    delta_y = owner_device // size_z % size_y - lax.axis_index("gy")
    delta_z = owner_device % size_z - lax.axis_index("gz")
    heading = jnp.where(
        delta_x != 0,
        (delta_x > 0).astype(jnp.int32),
        jnp.where(
            delta_y != 0, 2 + (delta_y > 0).astype(jnp.int32), 4 + (delta_z > 0).astype(jnp.int32)
        ),
    )
    bin_count = 6
    onehot = (
        (heading[:, None] == jnp.arange(bin_count, dtype=jnp.int32)[None, :]) & moving[:, None]
    ).astype(jnp.int32)
    earlier = jnp.sum((jnp.cumsum(onehot, axis=0) - onehot) * onehot, axis=1)
    outbox_slot = jnp.where(moving, heading * MOVE_CAP + earlier, bin_count * MOVE_CAP)
    outbox = (
        jnp.zeros((bin_count * MOVE_CAP,) + carried.shape[1:], jnp.float32)
        .at[outbox_slot]
        .set(carried, mode="drop")
    )
    outbound = outbox.reshape((3, 2, MOVE_CAP) + carried.shape[1:])
    came_x = padded_2(outbound[0], (("gx", 0),), 1)
    came_y = padded_2(outbound[1], (("gy", 0),), 1)
    came_z = padded_2(outbound[2], (("gz", 0),), 1)
    arrived = jnp.concatenate(
        [came_x[0], came_x[3], came_y[0], came_y[3], came_z[0], came_z[3]], axis=0
    )
    labels = arrived[:, 7, 0]
    arrive_place = jnp.where(labels > 0.5, labels.astype(jnp.int32) - 1, blocks)
    return staying.at[arrive_place].set(arrived[:, 0:7], mode="drop")


def per_device(
    position,
    velocity,
    particle_mass,
    send_first,
    neighbours_first,
    destination,
    send_second,
    neighbours_second,
):
    density, acceleration = sph_forces(position, particle_mass, send_first[0], neighbours_first)
    velocity = velocity + time_step * acceleration
    position = position + time_step * velocity
    fields = jnp.concatenate([position, velocity, particle_mass[:, None, :]], axis=1)
    shifted = migrate(fields, destination)
    position = shifted[:, 0:3]
    velocity = shifted[:, 3:6]
    moved_mass = shifted[:, 6]
    density, acceleration = sph_forces(position, moved_mass, send_second[0], neighbours_second)
    velocity = velocity + time_step * acceleration
    position = position + time_step * velocity
    return (position, velocity, density)


def solution(mesh):
    in_specs = (
        P(("gx", "gy", "gz"), None, None),
        P(("gx", "gy", "gz"), None, None),
        P(("gx", "gy", "gz"), None),
        P(("gx", "gy", "gz"), None, None),
        P(("gx", "gy", "gz"), None),
        P(("gx", "gy", "gz")),
        P(("gx", "gy", "gz"), None, None),
        P(("gx", "gy", "gz"), None),
    )
    out_specs = (
        P(("gx", "gy", "gz"), None, None),
        P(("gx", "gy", "gz"), None, None),
        P(("gx", "gy", "gz"), None),
    )
    return jax.shard_map(
        per_device, mesh=mesh, in_specs=in_specs, out_specs=out_specs, check_vma=False
    )
```
